32 devices in a mesh: group: 2 (over y), ctx: 4 (over z), head: 4 (over x, core).
Axes of the slice: x: 2, y: 2, z: 4, core: 2. Of those that a mesh axis runs over, the one named last changes fastest.
Arguments:
- head_input: bfloat16 [4096, 8192], P(('group', 'ctx'), 'head'), parts along dimension 0, may hold values from -6 to 6
- gate_input: bfloat16 [4096, 8192], P(('group', 'ctx'), 'head'), parts along dimension 0, may hold values from -40 to 40
- input_map: bfloat16 [4096, 2048], P(('group', 'ctx'), 'head'), parts along dimension 0, may hold values from -4 to 4
- output_map: bfloat16 [4096, 2048], P(('group', 'ctx'), 'head'), parts along dimension 0, may hold values from -4 to 4
- step_size: float32 [128, 4096], P('head', ('group', 'ctx')), parts along dimension 1, may hold values from 0.1 to 0.4
- decays: float32 [128, 4096], P('head', ('group', 'ctx')), parts along dimension 1, may hold values from 0.45 to 1
- bypass_scale: float32 [128], P('head'), may hold values from 1 to 4
- norm_gain: bfloat16 [8192], P('head'), may hold values from 0.099609375 to 1.8984375
- out_weight: bfloat16 [8192, 4096], P('head', 'ctx'), may hold values from -0.0625 to 0.0625
Outputs:
- layer_out: bfloat16 [4096, 4096], P(('group', 'ctx', 'head')), parts along dimension 0
The draws below stay inside these ranges and needn't reach their ends.
There are 2 independent parts, one for each index of `group`. The reference program is written for one: setup_inputs(seed, part) draws one part's arguments, and reference() takes and returns one part's arrays. A program takes and returns all parts, laid end to end along the dimension named above; an argument that names none is the same for every part. Nothing has to cross between parts.
All inputs are finite; a program needn't handle non-finite values.
Results may differ from the reference program's by a relative error of at most 0.014.
Values may be sent and summed in bfloat16 or wider, within the bound.
A program may use at most 128 MiB of HBM per device.

```python
import math
import jax
import jax.numpy as jnp
from jax import lax

HEADS = 128
HEADP = 64
STATE = 256
GROUPS = 8
DOUT = 4096
STRETCH = 128
TOKENS = 2048
N_HEAD = 4


def draw_decays(key, part):
    keys = jax.random.split(key, 6)
    fast_share = 0.5
    fast = jax.random.uniform(keys[0], (HEADS,)) < fast_share
    fast_rate = jnp.exp(jax.random.uniform(keys[1], (HEADS,), jnp.float32, math.log(1.0 / 50.0), math.log(1.0 / 30.0)))
    slow_rate = jnp.exp(jax.random.uniform(keys[2], (HEADS,), jnp.float32, math.log(0.01), math.log(0.3))) / TOKENS
    fading_speed = jnp.where(fast, fast_rate, slow_rate)
    approximate_guess = jnp.exp(jax.random.uniform(keys[3], (HEADS, TOKENS), jnp.float32, math.log(0.5), math.log(2.0)))
    spots = jax.random.randint(keys[4], (2,), 0, TOKENS)
    places = jnp.arange(TOKENS)
    masked_cells = (places == spots[0]) | (places == spots[1])
    fading_logs = jax.random.uniform(keys[5], (HEADS, 1), jnp.float32, 0.5, 0.8)
    segment_size = jnp.where(masked_cells[None, :], fading_logs, 1.0)
    return (jnp.exp(-fading_speed[:, None] * approximate_guess) * segment_size).astype(jnp.float32)


def draw_gate_input(key, part):
    keys = jax.random.split(key, 3)
    width = HEADS * HEADP
    base = jnp.clip(jax.random.normal(keys[0], (TOKENS, width), jnp.float32), -4.0, 4.0)
    column = jnp.exp(jax.random.uniform(keys[1], (width,), jnp.float32, math.log(0.3), math.log(3.0)))
    row = jnp.exp(jax.random.uniform(keys[2], (TOKENS, 1), jnp.float32, 0.0, math.log(3.0)))
    return (base * column[None, :] * row).astype(jnp.bfloat16)


def block_levels(stream_key, shape, cuts, low, high):
    gain, own = 1.0, jax.random.fold_in(stream_key, 6)
    for position, parts in cuts:
        heights = jnp.exp(jax.random.uniform(jax.random.fold_in(own, position), (parts,), jnp.float32, low / len(cuts), high / len(cuts)))
        gain = gain * jnp.repeat(heights, shape[position] // parts).reshape([-1 if axis == position else 1 for axis in range(len(shape))])
    return gain


def gaussian(rng, dims, deviation, reach, pieces=(), kind=jnp.bfloat16):
    loudness = block_levels(rng, dims, pieces, -0.22, 0.18) if pieces else 1.0
    entries = jax.random.normal(rng, dims, jnp.float32) * deviation * loudness
    return jnp.minimum(jnp.maximum(entries, -reach), reach).astype(kind)


def setup_inputs(seed: int = 0, part: int = 0) -> dict:
    arg_keys = jax.random.split(jax.random.key(seed), 10)
    own_keys = jax.random.split(jax.random.fold_in(arg_keys[9], part), 10)
    return {
        "head_input": gaussian(own_keys[0], (TOKENS, HEADS * HEADP), 1.0, 6.0, ((0, 4), (1, 4))),
        "gate_input": draw_gate_input(jax.random.fold_in(jax.random.fold_in(arg_keys[9], part), 71), part),
        "input_map": gaussian(own_keys[2], (TOKENS, GROUPS * STATE), 0.3, 4.0, ((0, 4), (1, 4))),
        "output_map": gaussian(own_keys[3], (TOKENS, GROUPS * STATE), 0.3, 4.0, ((0, 4), (1, 4))),
        "step_size": jnp.clip(jnp.exp(math.log(0.4) - 1.3862944 * jax.random.uniform(own_keys[4], (HEADS, TOKENS), jnp.float32) ** block_levels(own_keys[4], (HEADS, TOKENS), ((0, 4), (1, 4)), -0.2, 0.2)), 0.1, 0.4),
        "decays": draw_decays(jax.random.fold_in(jax.random.fold_in(arg_keys[9], part), 71), part),
        "bypass_scale": jnp.clip(jnp.exp(math.log(4.0) - 1.3862944 * jax.random.uniform(arg_keys[6], (HEADS,), jnp.float32) ** block_levels(arg_keys[6], (HEADS,), ((0, 4),), -0.2, 0.2)), 1.0, 4.0),
        "norm_gain": jnp.clip(1.0 + 0.18 * jax.random.normal(arg_keys[7], (HEADS * HEADP,), jnp.float32), 0.099609375, 1.8984375).astype(jnp.bfloat16),
        "out_weight": gaussian(arg_keys[8], (HEADS * HEADP, DOUT), (HEADS * HEADP) ** -0.5, 0.0625, ((0, 4), (1, 4))),
    }


def block_term_values(inputs, in_maps, out_maps, steps, decays):
    count, length, groups, per_group, channels = inputs.shape
    ramps = jnp.cumsum(jnp.log(decays), axis=-1)
    rows = lax.broadcasted_iota(jnp.int32, (length, length), 0)
    cols = lax.broadcasted_iota(jnp.int32, (length, length), 1)
    lower = rows >= cols
    spread = ramps[:, :, :, None] - ramps[:, :, None, :]
    within_decay = jnp.where(lower, jnp.exp(jnp.where(lower, spread, 0.0)), 0.0)
    scores = jnp.einsum('kqgn,ksgn->kgqs', out_maps.astype(jnp.float32), in_maps.astype(jnp.float32))
    mixing = within_decay.reshape(count, groups, per_group, length, length) * scores[:, :, None]
    mixing = mixing * steps.reshape(count, groups, per_group, 1, length)
    mixing = mixing.astype(jnp.bfloat16)
    within = jnp.einsum('kgjqs,ksgjp->kqgjp', mixing.astype(jnp.float32), inputs.astype(jnp.float32))
    tails = jnp.exp(ramps[:, :, -1:] - ramps) * steps
    tails = jnp.transpose(tails.reshape(count, groups, per_group, length), (0, 3, 1, 2))[..., None]
    weighted = (inputs.astype(jnp.float32) * tails).astype(jnp.bfloat16)
    block_state = jnp.einsum('ksgjp,ksgn->kgjpn', weighted.astype(jnp.float32), in_maps.astype(jnp.float32))
    accumulated_sums_list = jnp.exp(ramps[:, :, -1]).reshape(count, groups, per_group)
    entry = jnp.transpose(jnp.exp(ramps).reshape(count, groups, per_group, length), (0, 3, 1, 2))[..., None]
    return (within, block_state, accumulated_sums_list, entry)

def carried_terms(out_maps, entering, entry):
    carried = jnp.einsum('kqgn,kgjpn->kqgjp', out_maps.astype(jnp.float32), entering, precision=lax.Precision.HIGHEST)
    return carried * entry

def reference(head_input, gate_input, input_map, output_map, step_size, decays, bypass_scale, norm_gain, out_weight):
    per_group = HEADS // GROUPS
    blocks = TOKENS // STRETCH
    inputs = head_input.reshape(blocks, 1, STRETCH, GROUPS, per_group, HEADP)
    in_maps = input_map.reshape(blocks, 1, STRETCH, GROUPS, STATE)
    out_maps = output_map.reshape(blocks, 1, STRETCH, GROUPS, STATE)
    steps = jnp.transpose(step_size.reshape(HEADS, blocks, STRETCH), (1, 0, 2))[:, None]
    rates = jnp.transpose(decays.reshape(HEADS, blocks, STRETCH), (1, 0, 2))[:, None]
    skip = bypass_scale.reshape(GROUPS, per_group, 1)

    def advance(state, item):
        block_in, block_b, block_c, block_steps, block_rates = item
        within, block_state, accumulated_sums_list, entry = block_term_values(block_in, block_b, block_c, block_steps, block_rates)
        carried = carried_terms(block_c, state, entry)
        mamba_out = within + carried + skip * block_in.astype(jnp.float32)
        new_state = accumulated_sums_list[..., None, None] * state + block_state
        return (new_state, mamba_out[0])
    initial_state = jnp.zeros((1, GROUPS, per_group, HEADP, STATE), jnp.float32)
    final_state, outputs = lax.scan(advance, initial_state, (inputs, in_maps, out_maps, steps, rates))
    mamba_out = outputs.reshape(TOKENS, HEADS * HEADP)
    gated = mamba_out * jax.nn.silu(gate_input.astype(jnp.float32))
    grouped = gated.reshape(TOKENS, GROUPS, -1)
    factor = lax.rsqrt(lax.optimization_barrier(jnp.mean(grouped * grouped, axis=-1, keepdims=True)) + 1e-05)
    normed = ((grouped * factor).reshape(TOKENS, HEADS * HEADP) * norm_gain.astype(jnp.float32)).astype(jnp.bfloat16)
    span = HEADS * HEADP // N_HEAD
    summed = jnp.zeros((TOKENS, DOUT), jnp.float32)
    for index in range(N_HEAD):
        partial_value = jnp.dot(normed[:, index * span:(index + 1) * span], out_weight[index * span:(index + 1) * span], preferred_element_type=jnp.float32).astype(jnp.bfloat16)
        summed = summed + lax.optimization_barrier(partial_value).astype(jnp.float32)
    return summed.astype(jnp.bfloat16)
```

```python
import jax
import jax.numpy as jnp
from jax import lax
from jax.sharding import PartitionSpec as P

HEADP = 64
STATE = 256
STRETCH = 128


def carried_in(shard, axis):
    size, position = lax.axis_size(axis), lax.axis_index(axis)
    decay, state = shard
    hops = [(i, i + 1) for i in range(size - 1)]
    incoming = jnp.zeros_like(state)
    for hop in range(size - 1):
        total = (decay[..., None, None] * incoming + state).astype(jnp.bfloat16)
        incoming = lax.ppermute(total, axis, hops).astype(jnp.float32)
    return incoming


def block_term_values(inputs, in_maps, out_maps, steps, decays):
    count, length, groups, per_group, channels = inputs.shape
    ramps = jnp.cumsum(jnp.log(decays), axis=-1)
    rows = lax.broadcasted_iota(jnp.int32, (length, length), 0)
    cols = lax.broadcasted_iota(jnp.int32, (length, length), 1)
    lower = rows >= cols
    spread = ramps[:, :, :, None] - ramps[:, :, None, :]
    within_decay = jnp.where(lower, jnp.exp(jnp.where(lower, spread, 0.0)), 0.0)
    scores = jnp.einsum("kqgn,ksgn->kgqs", out_maps, in_maps, preferred_element_type=jnp.float32)
    mixing = within_decay.reshape(count, groups, per_group, length, length) * scores[:, :, None]
    mixing = mixing * steps.reshape(count, groups, per_group, 1, length)
    mixing = mixing.astype(jnp.bfloat16)
    within = jnp.einsum("kgjqs,ksgjp->kqgjp", mixing, inputs, preferred_element_type=jnp.float32)
    tails = jnp.exp(ramps[:, :, -1:] - ramps) * steps
    tails = jnp.transpose(tails.reshape(count, groups, per_group, length), (0, 3, 1, 2))[..., None]
    weighted = (inputs.astype(jnp.float32) * tails).astype(jnp.bfloat16)
    block_state = jnp.einsum(
        "ksgjp,ksgn->kgjpn", weighted, in_maps, preferred_element_type=jnp.float32
    )
    accumulated_sums_list = jnp.exp(ramps[:, :, -1]).reshape(count, groups, per_group)
    entry = jnp.transpose(jnp.exp(ramps).reshape(count, groups, per_group, length), (0, 3, 1, 2))[
        ..., None
    ]
    return (within, block_state, accumulated_sums_list, entry)


def shards(
    head_input,
    gate_input,
    input_map,
    output_map,
    step_size,
    decays,
    bypass_scale,
    norm_gain,
    out_weight,
):
    tok_rows, width = head_input.shape
    heads = step_size.shape[0]
    groups = input_map.shape[1] // STATE
    per_group = heads // groups
    blocks = tok_rows // STRETCH
    inputs = head_input.reshape(blocks, STRETCH, groups, per_group, HEADP)
    in_maps = input_map.reshape(blocks, STRETCH, groups, STATE)
    out_maps = output_map.reshape(blocks, STRETCH, groups, STATE)
    steps = jnp.transpose(step_size.reshape(heads, blocks, STRETCH), (1, 0, 2))
    rates = jnp.transpose(decays.reshape(heads, blocks, STRETCH), (1, 0, 2))
    within, block_state, accumulated_sums_list, entry = block_term_values(
        inputs, in_maps, out_maps, steps, rates
    )

    def advance(carry, item):
        state, lead = carry
        total, piece = item
        return ((total[..., None, None] * state + piece, total * lead), (state, lead))

    empty_state = jnp.zeros((groups, per_group, HEADP, STATE), jnp.float32)
    unit_decay = jnp.ones((groups, per_group), jnp.float32)
    (local_state, local_decay), (local_entering, leads) = lax.scan(
        advance, (empty_state, unit_decay), (accumulated_sums_list, block_state)
    )
    incoming = carried_in((local_decay, local_state), "ctx")
    entering = local_entering + leads[..., None, None] * incoming
    carried = (
        jnp.einsum(
            "kqgn,kgjpn->kqgjp",
            out_maps.astype(jnp.float32),
            entering,
            precision=lax.Precision.HIGHEST,
        )
        * entry
    )
    skip = bypass_scale.reshape(groups, per_group, 1)
    mamba_out = (within + carried + skip * inputs.astype(jnp.float32)).reshape(tok_rows, width)
    gated = mamba_out * jax.nn.silu(gate_input.astype(jnp.float32))
    grouped = gated.reshape(tok_rows, groups, -1)
    factor = lax.rsqrt(jnp.mean(grouped * grouped, axis=-1, keepdims=True) + 1e-05)
    normed = ((grouped * factor).reshape(tok_rows, width) * norm_gain.astype(jnp.float32)).astype(
        jnp.bfloat16
    )
    lanes = lax.axis_size("group")
    span = width // lanes
    mine = lax.dynamic_slice_in_dim(out_weight, lax.axis_index("group") * span, span, 0)
    whole = lax.all_gather(mine, ("group", "ctx"))
    whole = whole.reshape(lanes, lax.axis_size("ctx"), span, out_weight.shape[1])
    terms = jnp.einsum(
        "tgr,gcrn->tcn",
        normed.reshape(tok_rows, lanes, span),
        whole,
        preferred_element_type=jnp.float32,
    ).reshape(tok_rows, -1)
    summed = lax.psum_scatter(terms.astype(jnp.bfloat16), "head", scatter_dimension=0, tiled=True)
    return summed


def solution(mesh):
    return jax.shard_map(
        shards,
        mesh=mesh,
        in_specs=(
            P(("group", "ctx"), "head"),
            P(("group", "ctx"), "head"),
            P(("group", "ctx"), "head"),
            P(("group", "ctx"), "head"),
            P("head", ("group", "ctx")),
            P("head", ("group", "ctx")),
            P("head"),
            P("head"),
            P("head", "ctx"),
        ),
        out_specs=P(("group", "ctx", "head"), None),
        check_vma=False,
    )
```

```python
import functools

import jax
import jax.numpy as jnp
from jax import lax
from jax.experimental import pallas as pl
from jax.experimental.pallas import tpu as pltpu
from jax.sharding import PartitionSpec as P

HEADP = 64
STATE = 256
STRETCH = 128
PIECES = 2
QUARTERS = 4
MESH = pl.DeviceIdType.MESH
F32 = jnp.float32
BF16 = jnp.bfloat16


def rows_of(k, size):
    return pl.ds(pl.multiple_of(k * size, size), size)


def layer(
    sizes,
    x_ref,
    gate_ref,
    bm_ref,
    cm_ref,
    step_ref,
    dec_ref,
    skip_ref,
    gain_ref,
    w_ref,
    out_ref,
    wg,
    part,
    rs,
    y_ref,
    st,
    ent,
    inc,
    sbuf,
    normed,
    expander,
    ramp_t,
    rows_r,
    lead_ref,
    full_ref,
    local_sem,
    w_recv,
    up_send,
    down_send,
    side_send,
    st_send,
    st_recv,
    rs_send,
    rs_recv,
):
    lanes, ctx, peers = sizes
    tokens, width = x_ref.shape
    heads = step_ref.shape[0]
    groups = bm_ref.shape[1] // STATE
    blocks = tokens // STRETCH
    chunks, depth, cw = wg.shape[1:]
    share = lanes == 2 and chunks % 2 == 0
    line_chunks = chunks // 2 if share else chunks
    units = (ctx - 1) * line_chunks
    slots = units * PIECES
    span = depth // PIECES
    gw = width // groups
    qw = width // QUARTERS
    owned = tokens // peers
    y, z, me = lax.axis_index("group"), lax.axis_index("ctx"), lax.axis_index("head")
    above, below = z + 1 < ctx, z > 0
    other = {"group": 1 - y} if share else None

    barrier = pltpu.get_barrier_semaphore()

    @pl.when(above)
    def _():
        pl.semaphore_signal(barrier, inc=1, device_id={"ctx": z + 1}, device_id_type=MESH)

    @pl.when(below)
    def _():
        pl.semaphore_signal(barrier, inc=1, device_id={"ctx": z - 1}, device_id_type=MESH)

    if share:
        pl.semaphore_signal(barrier, inc=1, device_id=other, device_id_type=MESH)
    for d in range(1, peers):
        pl.semaphore_signal(
            barrier, inc=1, device_id={"head": lax.rem(me + d, peers)}, device_id_type=MESH
        )
    ends = jnp.where(above, 1, 0) + jnp.where(below, 1, 0)
    pl.semaphore_wait(barrier, peers - 1 + (1 if share else 0) + ends)

    def line_chunk(i):
        return 2 * i + y if share else i

    def piece(j, c, r):
        return wg.at[j, c, rows_of(r, span)]

    def send(src, j, c, r, sem, target):
        return pltpu.make_async_remote_copy(
            src_ref=src,
            dst_ref=piece(j, c, r),
            send_sem=sem.at[j, c, r],
            recv_sem=w_recv.at[j, c, r],
            device_id=target,
            device_id_type=MESH,
        )

    def own_piece(c, r):
        return w_ref.at[rows_of(r, span), rows_of(c, cw)]

    def arrived(j, c, r):
        send(piece(j, c, r), j, c, r, up_send, {"head": lax.rem(me + 1, peers)}).wait_recv()

    def own_sends(i, wait):
        c, r = line_chunk(lax.div(i, PIECES)), lax.rem(i, PIECES)
        for flag, sem, target in ((above, up_send, z + 1), (below, down_send, z - 1)):

            @pl.when(flag)
            def _():
                copy = send(own_piece(c, r), z, c, r, sem, {"ctx": target})
                if wait:
                    copy.wait_send()
                else:
                    copy.start()

    def each(count, body):
        def go(i, carry):
            body(i)
            return carry

        lax.fori_loop(0, count, go, 0)

    each(line_chunks * PIECES, lambda i: own_sends(i, False))

    def local_copy(c):
        return pltpu.make_async_copy(w_ref.at[:, rows_of(c, cw)], wg.at[z, c], local_sem.at[c])

    each(chunks, lambda c: local_copy(c).start())

    def service(slot, wait=False):
        unit, r = lax.div(slot, PIECES), lax.rem(slot, PIECES)
        s, c = lax.div(unit, line_chunks), line_chunk(lax.rem(unit, line_chunks))
        for j, valid, more, sem, target in (
            (z - 1 - s, z - 1 - s >= 0, above, up_send, z + 1),
            (z + 1 + s, z + 1 + s < ctx, below, down_send, z - 1),
        ):

            @pl.when(jnp.logical_and(valid, slot < slots))
            def _():
                if not wait:
                    arrived(j, c, r)

                @pl.when(more)
                def _():
                    copy = send(piece(j, c, r), j, c, r, sem, {"ctx": target})
                    if wait:
                        copy.wait_send()
                    else:
                        copy.start()

                if share:
                    copy = send(piece(j, c, r), j, c, r, side_send, other)
                    if wait:
                        copy.wait_send()
                    else:
                        copy.start()

    spots = lax.broadcasted_iota(jnp.int32, (heads, width), 1)
    owner = lax.broadcasted_iota(jnp.int32, (heads, width), 0)
    inside = jnp.logical_and(spots >= owner * HEADP, spots < owner * HEADP + HEADP)
    expander[...] = jnp.where(inside, 1.0, 0.0).astype(BF16)

    def spread(v, lo, size):
        high = v.astype(BF16)
        low = (v - high.astype(F32)).astype(BF16)
        e = expander[:, lo : lo + size]
        return jnp.dot(high, e, preferred_element_type=F32) + jnp.dot(
            low, e, preferred_element_type=F32
        )

    row_i = lax.broadcasted_iota(jnp.int32, (STRETCH, STRETCH), 0)
    col_i = lax.broadcasted_iota(jnp.int32, (STRETCH, STRETCH), 1)
    lower = row_i >= col_i
    nt = (((1,), (1,)), ((), ()))
    tn = (((0,), (0,)), ((), ()))

    st[...] = jnp.zeros_like(st)

    def states(k, lead):
        rows = rows_of(k, STRETCH)
        low_tri = jnp.where(lower, 1.0, 0.0).astype(F32)
        eye = jnp.where(row_i == col_i, 1.0, 0.0).astype(F32)
        logd = jnp.log(dec_ref[:, rows])
        logs = jnp.log(step_ref[:, rows])
        exact = functools.partial(
            lax.dot_general,
            dimension_numbers=nt,
            precision=lax.Precision.HIGHEST,
            preferred_element_type=F32,
        )
        ramp = exact(logd, low_tri)
        rt = exact(low_tri, logd)
        st_t = exact(eye, logs)
        rows_r[k] = ramp - logs
        ramp_t[k] = rt
        lead_ref[k] = lead
        end = rt[STRETCH - 1 : STRETCH, :]
        tails = jnp.exp(end - (rt - st_t))
        total = jnp.broadcast_to(jnp.exp(end), (8, heads))
        for g in range(groups):
            cols = slice(g * gw, (g + 1) * gw)
            weighted = (x_ref[rows, cols].astype(F32) * spread(tails, g * gw, gw)).astype(BF16)
            made = lax.dot_general(
                bm_ref[rows, g * STATE : (g + 1) * STATE],
                weighted,
                tn,
                preferred_element_type=F32,
            )
            old = st[:, cols]
            ent[k, :, cols] = old.astype(BF16)
            st[:, cols] = spread(total, g * gw, gw)[0:1] * old + made
        return lead + jnp.broadcast_to(end, (8, heads))

    lead = lax.fori_loop(0, blocks, states, jnp.zeros((8, heads), F32))
    full_ref[...] = jnp.exp(lead)

    def state_copy(q):
        return pltpu.make_async_remote_copy(
            src_ref=sbuf.at[q],
            dst_ref=inc.at[q],
            send_sem=st_send.at[q],
            recv_sem=st_recv.at[q],
            device_id={"ctx": z + 1},
            device_id_type=MESH,
        )

    @pl.when(z == 0)
    def _():
        for q in range(QUARTERS):
            inc[q] = jnp.zeros_like(inc[q])
            sbuf[q] = st[:, q * qw : (q + 1) * qw].astype(BF16)

            @pl.when(above)
            def _():
                state_copy(q).start()

    service(0)

    def chain():
        for q in range(QUARTERS):
            pltpu.make_async_remote_copy(
                src_ref=sbuf.at[q],
                dst_ref=inc.at[q],
                send_sem=st_send.at[q],
                recv_sem=st_recv.at[q],
                device_id={"ctx": z - 1},
                device_id_type=MESH,
            ).wait_recv()

            @pl.when(above)
            def _():
                fall = spread(full_ref[...], q * qw, qw)[0:1]
                held = st[:, q * qw : (q + 1) * qw]
                sbuf[q] = (fall * inc[q].astype(F32) + held).astype(BF16)
                state_copy(q).start()

    half = lax.broadcasted_iota(jnp.int32, (STRETCH, 2 * HEADP), 1) < HEADP
    keep_lo = jnp.where(half, 1.0, 0.0).astype(BF16)
    keep_hi = jnp.where(half, 0.0, 1.0).astype(BF16)
    per_group = heads // groups

    def own_block(k, carry):
        rows = rows_of(k, STRETCH)
        rt = ramp_t[k]
        rr = rows_r[k]
        entry = jnp.exp(rt)
        for g in range(groups):
            c_map = cm_ref[rows, g * STATE : (g + 1) * STATE]
            b_map = bm_ref[rows, g * STATE : (g + 1) * STATE]
            scores = lax.dot_general(c_map, b_map, nt, preferred_element_type=F32)
            cols = slice(g * gw, (g + 1) * gw)
            skip = spread(jnp.broadcast_to(skip_ref[...], (8, heads)), g * gw, gw)[0:1]
            y_ref[rows, cols] = (
                jnp.dot(c_map, ent[k, :, cols], preferred_element_type=F32)
                * spread(entry, g * gw, gw)
                + skip * x_ref[rows, cols].astype(F32)
            )
            for pair in range(per_group // 2):
                mixes = []
                for h in (g * per_group + 2 * pair, g * per_group + 2 * pair + 1):
                    fade = jnp.where(lower, rt[:, h : h + 1] - rr[h : h + 1, :], -1e30)
                    mixes.append((scores * jnp.exp(fade)).astype(BF16))
                at = slice(g * gw + pair * 2 * HEADP, g * gw + (pair + 1) * 2 * HEADP)
                both = x_ref[rows, at]
                y_ref[rows, at] += jnp.dot(
                    jnp.concatenate(mixes, axis=1),
                    jnp.concatenate([both * keep_lo, both * keep_hi], axis=0),
                    preferred_element_type=F32,
                )

        @pl.when(jnp.logical_and(below, jnp.minimum(z - 1, blocks - 1) == k))
        def _():
            chain()

        service(1 + k)
        return carry

    lax.fori_loop(0, blocks, own_block, 0)

    def finish_block(k, carry):
        rows = rows_of(k, STRETCH)
        reach = jnp.exp(ramp_t[k] + lead_ref[k, 0:1])
        squares = [jnp.zeros((STRETCH, 1), F32) for _ in range(groups)]
        for q in range(QUARTERS):
            g = q * qw // gw
            cols = slice(q * qw, (q + 1) * qw)
            carried = jnp.dot(
                cm_ref[rows, g * STATE : (g + 1) * STATE], inc[q], preferred_element_type=F32
            )
            gate = gate_ref[rows, cols].astype(F32)
            gated = (y_ref[rows, cols] + carried * spread(reach, q * qw, qw)) * (
                gate / (1.0 + jnp.exp(-gate))
            )
            y_ref[rows, cols] = gated
            squares[g] = squares[g] + jnp.sum(gated * gated, axis=1, keepdims=True)
        for g in range(groups):
            cols = slice(g * gw, (g + 1) * gw)
            factor = lax.rsqrt(squares[g] / gw + 1e-05)
            normed[rows, cols] = (y_ref[rows, cols] * factor * gain_ref[:, cols].astype(F32)).astype(
                BF16
            )

        @pl.when(lax.rem(k, 2) == 1)
        def _():
            service(1 + blocks + lax.div(k, 2))

        return carry

    lax.fori_loop(0, blocks, finish_block, 0)
    first = 1 + blocks + blocks // 2

    def partial_copy(d, j, c):
        peer = lax.rem(me + d, peers)
        return pltpu.make_async_remote_copy(
            src_ref=part.at[j, c, rows_of(peer, owned)],
            dst_ref=rs.at[d - 1, j, c],
            send_sem=rs_send.at[d - 1, j, c],
            recv_sem=rs_recv.at[d - 1, j, c],
            device_id={"head": peer},
            device_id_type=MESH,
        )

    entries = max(chunks, 4 if share else 2)

    def locate(v, e):
        own = v == 0
        line = e < 2
        unit = jnp.where(line, v - 1, v - 2)
        known = jnp.logical_and(unit >= 0, unit < units)
        safe = jnp.where(known, unit, 0)
        s, i = lax.div(safe, line_chunks), lax.rem(safe, line_chunks)
        j = jnp.where(lax.rem(e, 2) == 0, z - 1 - s, z + 1 + s)
        if share:
            c = jnp.where(line, 2 * i + y, 2 * i + 1 - y)
        else:
            c = i
        known = jnp.logical_and(known, e < (4 if share else 2))
        known = jnp.logical_and(known, jnp.logical_and(j >= 0, j < ctx))
        valid = jnp.where(own, e < chunks, known)
        return own, line, jnp.where(own, z, j), jnp.where(own, e, c), valid

    def project(v, e):
        own, line, j, c, valid = locate(v, e)

        @pl.when(jnp.logical_and(valid, own))
        def _():
            local_copy(c).wait()

        @pl.when(jnp.logical_and(valid, jnp.logical_not(jnp.logical_or(own, line))))
        def _():
            for r in range(PIECES):
                arrived(j, c, r)

        @pl.when(valid)
        def _():
            part[j, c] = jnp.dot(normed[...], wg[j, c], preferred_element_type=F32).astype(BF16)
            for d in range(1, peers):
                partial_copy(d, j, c).start()

    def collect(v, e):
        own, line, j, c, valid = locate(v, e)

        @pl.when(valid)
        def _():
            total = part[j, c, rows_of(me, owned)].astype(F32)
            for d in range(1, peers):
                partial_copy(d, j, c).wait_recv()
                total = total + rs[d - 1, j, c].astype(F32)
            out_ref[:, rows_of(j * chunks + c, cw)] = total.astype(BF16)

    def rounds(v):
        @pl.when(jnp.logical_and(v >= 1, v <= units))
        def _():
            for r in range(PIECES):
                slot = (v - 1) * PIECES + r

                @pl.when(slot >= first)
                def _():
                    service(slot)

        each(entries, lambda e: project(v, e))

    each(units + 2, rounds)
    each(units + 2, lambda v: each(entries, lambda e: collect(v, e)))

    each(line_chunks * PIECES, lambda i: own_sends(i, True))
    each(slots, lambda i: service(i, True))

    @pl.when(above)
    def _():
        for q in range(QUARTERS):
            state_copy(q).wait_send()

    def sent(u):
        j, c = lax.div(u, chunks), lax.rem(u, chunks)
        for d in range(1, peers):
            partial_copy(d, j, c).wait_send()

    each(ctx * chunks, sent)


def shards(
    sizes,
    head_input,
    gate_input,
    input_map,
    output_map,
    step_size,
    decays,
    bypass_scale,
    norm_gain,
    out_weight,
):
    lanes, ctx, peers = sizes
    tokens, width = head_input.shape
    heads = step_size.shape[0]
    blocks = tokens // STRETCH
    depth, cols = out_weight.shape
    cw = min(cols, 256)
    chunks = cols // cw
    owned = tokens // peers
    dma = pltpu.SemaphoreType.DMA
    vmem = pl.BlockSpec(memory_space=pltpu.VMEM)
    return pl.pallas_call(
        functools.partial(layer, sizes),
        out_shape=jax.ShapeDtypeStruct((owned, ctx * cols), BF16),
        in_specs=[vmem] * 8 + [pl.BlockSpec(memory_space=pl.ANY)],
        out_specs=vmem,
        scratch_shapes=[
            pltpu.VMEM((ctx, chunks, depth, cw), BF16),
            pltpu.VMEM((ctx, chunks, tokens, cw), BF16),
            pltpu.VMEM((peers - 1, ctx, chunks, owned, cw), BF16),
            pltpu.VMEM((tokens, width), F32),
            pltpu.VMEM((STATE, width), F32),
            pltpu.VMEM((blocks, STATE, width), BF16),
            pltpu.VMEM((QUARTERS, STATE, width // QUARTERS), BF16),
            pltpu.VMEM((QUARTERS, STATE, width // QUARTERS), BF16),
            pltpu.VMEM((tokens, width), BF16),
            pltpu.VMEM((heads, width), BF16),
            pltpu.VMEM((blocks, STRETCH, heads), F32),
            pltpu.VMEM((blocks, heads, STRETCH), F32),
            pltpu.VMEM((blocks, 8, heads), F32),
            pltpu.VMEM((8, heads), F32),
            dma((chunks,)),
            dma((ctx, chunks, PIECES)),
            dma((ctx, chunks, PIECES)),
            dma((ctx, chunks, PIECES)),
            dma((ctx, chunks, PIECES)),
            dma((QUARTERS,)),
            dma((QUARTERS,)),
            dma((peers - 1, ctx, chunks)),
            dma((peers - 1, ctx, chunks)),
        ],
        compiler_params=pltpu.CompilerParams(
            collective_id=0, has_side_effects=True, vmem_limit_bytes=60 << 20
        ),
    )(
        head_input,
        gate_input,
        input_map,
        output_map,
        step_size,
        decays,
        bypass_scale.reshape(1, heads),
        norm_gain.reshape(1, width),
        out_weight,
    )


def solution(mesh):
    sizes = (mesh.shape["group"], mesh.shape["ctx"], mesh.shape["head"])
    return jax.shard_map(
        functools.partial(shards, sizes),
        mesh=mesh,
        in_specs=(
            P(("group", "ctx"), "head"),
            P(("group", "ctx"), "head"),
            P(("group", "ctx"), "head"),
            P(("group", "ctx"), "head"),
            P("head", ("group", "ctx")),
            P("head", ("group", "ctx")),
            P("head"),
            P("head"),
            P("head", "ctx"),
        ),
        out_specs=P(("group", "ctx", "head"), None),
        check_vma=False,
    )
```

```python
import functools

import jax
import jax.numpy as jnp
from jax import lax
from jax.experimental import pallas as pl
from jax.experimental.pallas import tpu as pltpu
from jax.sharding import PartitionSpec as P

HEADP = 64
STATE = 256
STRETCH = 128
PIECES = 4
DELAY = 2
QUARTERS = 4
MESH = pl.DeviceIdType.MESH
F32 = jnp.float32
BF16 = jnp.bfloat16


def rows_of(k, size):
    return pl.ds(pl.multiple_of(k * size, size), size)


def layer(
    sizes,
    x_ref,
    gate_ref,
    bm_ref,
    cm_ref,
    step_ref,
    dec_ref,
    skip_ref,
    gain_ref,
    w_ref,
    out_ref,
    wg,
    part,
    rs,
    y_ref,
    st,
    ent,
    inc,
    sbuf,
    normed,
    expander,
    ramp_t,
    rows_r,
    lead_ref,
    full_ref,
    local_sem,
    w_recv,
    up_send,
    down_send,
    side_send,
    st_send,
    st_recv,
    rs_send,
    rs_recv,
):
    lanes, ctx, peers = sizes
    tokens, width = x_ref.shape
    heads = step_ref.shape[0]
    groups = bm_ref.shape[1] // STATE
    blocks = tokens // STRETCH
    chunks, depth, cw = wg.shape[1:]
    share = lanes == 2 and chunks % 2 == 0
    line_chunks = chunks // 2 if share else chunks
    units = (ctx - 1) * line_chunks
    slots = units * PIECES
    span = depth // PIECES
    gw = width // groups
    qw = width // QUARTERS
    owned = tokens // peers
    y, z, me = lax.axis_index("group"), lax.axis_index("ctx"), lax.axis_index("head")
    above, below = z + 1 < ctx, z > 0
    other = {"group": 1 - y} if share else None

    barrier = pltpu.get_barrier_semaphore()

    @pl.when(above)
    def _():
        pl.semaphore_signal(barrier, inc=1, device_id={"ctx": z + 1}, device_id_type=MESH)

    @pl.when(below)
    def _():
        pl.semaphore_signal(barrier, inc=1, device_id={"ctx": z - 1}, device_id_type=MESH)

    if share:
        pl.semaphore_signal(barrier, inc=1, device_id=other, device_id_type=MESH)
    for d in range(1, peers):
        pl.semaphore_signal(
            barrier, inc=1, device_id={"head": lax.rem(me + d, peers)}, device_id_type=MESH
        )
    ends = jnp.where(above, 1, 0) + jnp.where(below, 1, 0)
    pl.semaphore_wait(barrier, peers - 1 + (1 if share else 0) + ends)

    def line_chunk(i):
        return 2 * i + y if share else i

    def piece(j, c, r):
        return wg.at[j, c, rows_of(r, span)]

    def send(src, j, c, r, sem, target):
        return pltpu.make_async_remote_copy(
            src_ref=src,
            dst_ref=piece(j, c, r),
            send_sem=sem.at[j, c, r],
            recv_sem=w_recv.at[j, c, r],
            device_id=target,
            device_id_type=MESH,
        )

    def own_piece(c, r):
        return w_ref.at[rows_of(r, span), rows_of(c, cw)]

    def arrived(j, c, r):
        send(piece(j, c, r), j, c, r, up_send, {"head": lax.rem(me + 1, peers)}).wait_recv()

    own_count = line_chunks * PIECES
    early = jnp.where(z == ctx - 2, own_count // 2, 0)

    def own_send(i, flag, sem, target, wait=False):
        c, r = line_chunk(lax.div(i, PIECES)), lax.rem(i, PIECES)

        @pl.when(flag)
        def _():
            copy = send(own_piece(c, r), z, c, r, sem, {"ctx": target})
            if wait:
                copy.wait_send()
            else:
                copy.start()

    def own_down(i, wait=False):
        own_send(i, below, down_send, z - 1, wait)

    def own_up(i, first_part):
        now = (i < early) if first_part else (i >= early)
        own_send(i, jnp.logical_and(above, now), up_send, z + 1)

    def each(count, body):
        def go(i, carry):
            body(i)
            return carry

        lax.fori_loop(0, count, go, 0)

    each(own_count, own_down)
    each(own_count, lambda i: own_up(i, True))

    def local_copy(c):
        return pltpu.make_async_copy(w_ref.at[:, rows_of(c, cw)], wg.at[z, c], local_sem.at[c])

    each(chunks, lambda c: local_copy(c).start())

    late = jnp.where(z == ctx - 1, 0, DELAY)

    def service(at, wait=False):
        for up in (True, False):
            slot = at - late * PIECES if up and not wait else at
            fits = jnp.logical_and(slot >= 0, slot < slots)
            slot = jnp.where(fits, slot, 0)
            unit, r = lax.div(slot, PIECES), lax.rem(slot, PIECES)
            s, c = lax.div(unit, line_chunks), line_chunk(lax.rem(unit, line_chunks))
            if up:
                j, more, sem, target = z - 1 - s, above, up_send, z + 1
            else:
                j, more, sem, target = z + 1 + s, below, down_send, z - 1
            valid = jnp.logical_and(j >= 0, j < ctx)

            @pl.when(jnp.logical_and(valid, fits))
            def _():
                if not wait:
                    arrived(j, c, r)

                @pl.when(more)
                def _():
                    copy = send(piece(j, c, r), j, c, r, sem, {"ctx": target})
                    if wait:
                        copy.wait_send()
                    else:
                        copy.start()

                if share:
                    copy = send(piece(j, c, r), j, c, r, side_send, other)
                    if wait:
                        copy.wait_send()
                    else:
                        copy.start()

    spots = lax.broadcasted_iota(jnp.int32, (heads, width), 1)
    owner = lax.broadcasted_iota(jnp.int32, (heads, width), 0)
    inside = jnp.logical_and(spots >= owner * HEADP, spots < owner * HEADP + HEADP)
    expander[...] = jnp.where(inside, 1.0, 0.0).astype(BF16)

    def spread(v, lo, size):
        high = v.astype(BF16)
        low = (v - high.astype(F32)).astype(BF16)
        e = expander[:, lo : lo + size]
        return jnp.dot(high, e, preferred_element_type=F32) + jnp.dot(
            low, e, preferred_element_type=F32
        )

    row_i = lax.broadcasted_iota(jnp.int32, (STRETCH, STRETCH), 0)
    col_i = lax.broadcasted_iota(jnp.int32, (STRETCH, STRETCH), 1)
    lower = row_i >= col_i
    nt = (((1,), (1,)), ((), ()))
    tn = (((0,), (0,)), ((), ()))

    st[...] = jnp.zeros_like(st)

    def states(k, lead):
        rows = rows_of(k, STRETCH)
        low_tri = jnp.where(lower, 1.0, 0.0).astype(F32)
        eye = jnp.where(row_i == col_i, 1.0, 0.0).astype(F32)
        logd = jnp.log(dec_ref[:, rows])
        logs = jnp.log(step_ref[:, rows])
        exact = functools.partial(
            lax.dot_general,
            dimension_numbers=nt,
            precision=lax.Precision.HIGHEST,
            preferred_element_type=F32,
        )
        ramp = exact(logd, low_tri)
        rt = exact(low_tri, logd)
        st_t = exact(eye, logs)
        rows_r[k] = ramp - logs
        ramp_t[k] = rt
        lead_ref[k] = lead
        end = rt[STRETCH - 1 : STRETCH, :]
        tails = jnp.exp(end - (rt - st_t))
        total = jnp.broadcast_to(jnp.exp(end), (8, heads))
        for g in range(groups):
            cols = slice(g * gw, (g + 1) * gw)
            weighted = (x_ref[rows, cols].astype(F32) * spread(tails, g * gw, gw)).astype(BF16)
            made = lax.dot_general(
                bm_ref[rows, g * STATE : (g + 1) * STATE],
                weighted,
                tn,
                preferred_element_type=F32,
            )
            old = st[:, cols]
            ent[k, :, cols] = old.astype(BF16)
            st[:, cols] = spread(total, g * gw, gw)[0:1] * old + made
        return lead + jnp.broadcast_to(end, (8, heads))

    lead = lax.fori_loop(0, blocks, states, jnp.zeros((8, heads), F32))
    full_ref[...] = jnp.exp(lead)

    def state_copy(q):
        return pltpu.make_async_remote_copy(
            src_ref=sbuf.at[q],
            dst_ref=inc.at[q],
            send_sem=st_send.at[q],
            recv_sem=st_recv.at[q],
            device_id={"ctx": z + 1},
            device_id_type=MESH,
        )

    @pl.when(z == 0)
    def _():
        for q in range(QUARTERS):
            inc[q] = jnp.zeros_like(inc[q])
            sbuf[q] = st[:, q * qw : (q + 1) * qw].astype(BF16)

            @pl.when(above)
            def _():
                state_copy(q).start()

        each(own_count, lambda i: own_up(i, False))

    def chain():
        for q in range(QUARTERS):
            pltpu.make_async_remote_copy(
                src_ref=sbuf.at[q],
                dst_ref=inc.at[q],
                send_sem=st_send.at[q],
                recv_sem=st_recv.at[q],
                device_id={"ctx": z - 1},
                device_id_type=MESH,
            ).wait_recv()

            @pl.when(above)
            def _():
                fall = spread(full_ref[...], q * qw, qw)[0:1]
                held = st[:, q * qw : (q + 1) * qw]
                sbuf[q] = (fall * inc[q].astype(F32) + held).astype(BF16)
                state_copy(q).start()

    half = lax.broadcasted_iota(jnp.int32, (STRETCH, 2 * HEADP), 1) < HEADP
    keep_lo = jnp.where(half, 1.0, 0.0).astype(BF16)
    keep_hi = jnp.where(half, 0.0, 1.0).astype(BF16)
    per_group = heads // groups

    def own_block(k, carry):
        rows = rows_of(k, STRETCH)
        rt = ramp_t[k]
        rr = rows_r[k]
        entry = jnp.exp(rt)
        for g in range(groups):
            c_map = cm_ref[rows, g * STATE : (g + 1) * STATE]
            b_map = bm_ref[rows, g * STATE : (g + 1) * STATE]
            scores = lax.dot_general(c_map, b_map, nt, preferred_element_type=F32)
            cols = slice(g * gw, (g + 1) * gw)
            skip = spread(jnp.broadcast_to(skip_ref[...], (8, heads)), g * gw, gw)[0:1]
            y_ref[rows, cols] = (
                jnp.dot(c_map, ent[k, :, cols], preferred_element_type=F32)
                * spread(entry, g * gw, gw)
                + skip * x_ref[rows, cols].astype(F32)
            )
            for pair in range(per_group // 2):
                mixes = []
                for h in (g * per_group + 2 * pair, g * per_group + 2 * pair + 1):
                    fade = jnp.where(lower, rt[:, h : h + 1] - rr[h : h + 1, :], -1e30)
                    mixes.append((scores * jnp.exp(fade)).astype(BF16))
                at = slice(g * gw + pair * 2 * HEADP, g * gw + (pair + 1) * 2 * HEADP)
                both = x_ref[rows, at]
                y_ref[rows, at] += jnp.dot(
                    jnp.concatenate(mixes, axis=1),
                    jnp.concatenate([both * keep_lo, both * keep_hi], axis=0),
                    preferred_element_type=F32,
                )

        return carry

    lax.fori_loop(0, blocks, own_block, 0)
    service(0)
    service(1)

    @pl.when(below)
    def _():
        chain()
        each(own_count, lambda i: own_up(i, False))

    def finish_block(k, carry):
        rows = rows_of(k, STRETCH)
        reach = jnp.exp(ramp_t[k] + lead_ref[k, 0:1])
        squares = [jnp.zeros((STRETCH, 1), F32) for _ in range(groups)]
        for q in range(QUARTERS):
            g = q * qw // gw
            cols = slice(q * qw, (q + 1) * qw)
            carried = jnp.dot(
                cm_ref[rows, g * STATE : (g + 1) * STATE], inc[q], preferred_element_type=F32
            )
            gate = gate_ref[rows, cols].astype(F32)
            gated = (y_ref[rows, cols] + carried * spread(reach, q * qw, qw)) * (
                gate / (1.0 + jnp.exp(-gate))
            )
            y_ref[rows, cols] = gated
            squares[g] = squares[g] + jnp.sum(gated * gated, axis=1, keepdims=True)
        for g in range(groups):
            cols = slice(g * gw, (g + 1) * gw)
            factor = lax.rsqrt(squares[g] / gw + 1e-05)
            normed[rows, cols] = (y_ref[rows, cols] * factor * gain_ref[:, cols].astype(F32)).astype(
                BF16
            )

        service(2 + k)
        return carry

    lax.fori_loop(0, blocks, finish_block, 0)
    first = 2 + blocks

    def partial_copy(d, j, c):
        peer = lax.rem(me + d, peers)
        return pltpu.make_async_remote_copy(
            src_ref=part.at[j, c, rows_of(peer, owned)],
            dst_ref=rs.at[d - 1, j, c],
            send_sem=rs_send.at[d - 1, j, c],
            recv_sem=rs_recv.at[d - 1, j, c],
            device_id={"head": peer},
            device_id_type=MESH,
        )

    entries = max(chunks, 4 if share else 2)

    def locate(v, e):
        own = v == 0
        line = e < 2
        rising = lax.rem(e, 2) == 0
        unit = jnp.where(line, v - 1, v - 2) - jnp.where(rising, late, 0)
        known = jnp.logical_and(unit >= 0, unit < units)
        safe = jnp.where(known, unit, 0)
        s, i = lax.div(safe, line_chunks), lax.rem(safe, line_chunks)
        j = jnp.where(rising, z - 1 - s, z + 1 + s)
        if share:
            c = jnp.where(line, 2 * i + y, 2 * i + 1 - y)
        else:
            c = i
        known = jnp.logical_and(known, e < (4 if share else 2))
        known = jnp.logical_and(known, jnp.logical_and(j >= 0, j < ctx))
        valid = jnp.where(own, e < chunks, known)
        return own, line, jnp.where(own, z, j), jnp.where(own, e, c), valid

    def project(v, e):
        own, line, j, c, valid = locate(v, e)

        @pl.when(jnp.logical_and(valid, own))
        def _():
            local_copy(c).wait()

        @pl.when(jnp.logical_and(valid, jnp.logical_not(jnp.logical_or(own, line))))
        def _():
            for r in range(PIECES):
                arrived(j, c, r)

        @pl.when(valid)
        def _():
            part[j, c] = jnp.dot(normed[...], wg[j, c], preferred_element_type=F32).astype(BF16)
            for d in range(1, peers):
                partial_copy(d, j, c).start()

    def collect(v, e):
        own, line, j, c, valid = locate(v, e)

        @pl.when(valid)
        def _():
            total = part[j, c, rows_of(me, owned)].astype(F32)
            for d in range(1, peers):
                partial_copy(d, j, c).wait_recv()
                total = total + rs[d - 1, j, c].astype(F32)
            out_ref[:, rows_of(j * chunks + c, cw)] = total.astype(BF16)

    def rounds(v):
        @pl.when(jnp.logical_and(v >= 1, v <= units + DELAY))
        def _():
            for r in range(PIECES):
                slot = (v - 1) * PIECES + r

                @pl.when(slot >= first)
                def _():
                    service(slot)

        each(entries, lambda e: project(v, e))

    each(units + 2 + DELAY, rounds)
    each(units + 2 + DELAY, lambda v: each(entries, lambda e: collect(v, e)))

    each(own_count, lambda i: own_down(i, True))
    each(own_count, lambda i: own_send(i, above, up_send, z + 1, True))
    each(slots, lambda i: service(i, True))

    @pl.when(above)
    def _():
        for q in range(QUARTERS):
            state_copy(q).wait_send()

    def sent(u):
        j, c = lax.div(u, chunks), lax.rem(u, chunks)
        for d in range(1, peers):
            partial_copy(d, j, c).wait_send()

    each(ctx * chunks, sent)


def shards(
    sizes,
    head_input,
    gate_input,
    input_map,
    output_map,
    step_size,
    decays,
    bypass_scale,
    norm_gain,
    out_weight,
):
    lanes, ctx, peers = sizes
    tokens, width = head_input.shape
    heads = step_size.shape[0]
    blocks = tokens // STRETCH
    depth, cols = out_weight.shape
    cw = min(cols, 256)
    chunks = cols // cw
    owned = tokens // peers
    dma = pltpu.SemaphoreType.DMA
    vmem = pl.BlockSpec(memory_space=pltpu.VMEM)
    return pl.pallas_call(
        functools.partial(layer, sizes),
        out_shape=jax.ShapeDtypeStruct((owned, ctx * cols), BF16),
        in_specs=[vmem] * 8 + [pl.BlockSpec(memory_space=pl.ANY)],
        out_specs=vmem,
        scratch_shapes=[
            pltpu.VMEM((ctx, chunks, depth, cw), BF16),
            pltpu.VMEM((ctx, chunks, tokens, cw), BF16),
            pltpu.VMEM((peers - 1, ctx, chunks, owned, cw), BF16),
            pltpu.VMEM((tokens, width), F32),
            pltpu.VMEM((STATE, width), F32),
            pltpu.VMEM((blocks, STATE, width), BF16),
            pltpu.VMEM((QUARTERS, STATE, width // QUARTERS), BF16),
            pltpu.VMEM((QUARTERS, STATE, width // QUARTERS), BF16),
            pltpu.VMEM((tokens, width), BF16),
            pltpu.VMEM((heads, width), BF16),
            pltpu.VMEM((blocks, STRETCH, heads), F32),
            pltpu.VMEM((blocks, heads, STRETCH), F32),
            pltpu.VMEM((blocks, 8, heads), F32),
            pltpu.VMEM((8, heads), F32),
            dma((chunks,)),
            dma((ctx, chunks, PIECES)),
            dma((ctx, chunks, PIECES)),
            dma((ctx, chunks, PIECES)),
            dma((ctx, chunks, PIECES)),
            dma((QUARTERS,)),
            dma((QUARTERS,)),
            dma((peers - 1, ctx, chunks)),
            dma((peers - 1, ctx, chunks)),
        ],
        compiler_params=pltpu.CompilerParams(
            collective_id=0, has_side_effects=True, vmem_limit_bytes=60 << 20
        ),
    )(
        head_input,
        gate_input,
        input_map,
        output_map,
        step_size,
        decays,
        bypass_scale.reshape(1, heads),
        norm_gain.reshape(1, width),
        out_weight,
    )


def solution(mesh):
    sizes = (mesh.shape["group"], mesh.shape["ctx"], mesh.shape["head"])
    return jax.shard_map(
        functools.partial(shards, sizes),
        mesh=mesh,
        in_specs=(
            P(("group", "ctx"), "head"),
            P(("group", "ctx"), "head"),
            P(("group", "ctx"), "head"),
            P(("group", "ctx"), "head"),
            P("head", ("group", "ctx")),
            P("head", ("group", "ctx")),
            P("head"),
            P("head"),
            P("head", "ctx"),
        ),
        out_specs=P(("group", "ctx", "head"), None),
        check_vma=False,
    )
```

```python
import functools

import jax
import jax.numpy as jnp
from jax import lax
from jax.experimental import pallas as pl
from jax.experimental.pallas import tpu as pltpu
from jax.sharding import PartitionSpec as P

HEADP = 64
STATE = 256
STRETCH = 128
PIECES = 4
DELAY = 2
QUARTERS = 4
MESH = pl.DeviceIdType.MESH
F32 = jnp.float32
BF16 = jnp.bfloat16


def rows_of(k, size):
    return pl.ds(pl.multiple_of(k * size, size), size)


def layer(
    sizes,
    x_ref,
    gate_ref,
    bm_ref,
    cm_ref,
    step_ref,
    dec_ref,
    skip_ref,
    gain_ref,
    w_ref,
    out_ref,
    wg,
    part,
    rs,
    y_ref,
    st,
    ent,
    inc,
    sbuf,
    normed,
    expander,
    ramp_t,
    rows_r,
    lead_ref,
    full_ref,
    local_sem,
    w_recv,
    up_send,
    down_send,
    side_send,
    st_send,
    st_recv,
    rs_send,
    rs_recv,
):
    lanes, ctx, peers = sizes
    tokens, width = x_ref.shape
    heads = step_ref.shape[0]
    groups = bm_ref.shape[1] // STATE
    blocks = tokens // STRETCH
    chunks, depth, cw = wg.shape[1:]
    share = lanes == 2 and chunks % 2 == 0
    line_chunks = chunks // 2 if share else chunks
    units = (ctx - 1) * line_chunks
    slots = units * PIECES
    span = depth // PIECES
    gw = width // groups
    qw = width // QUARTERS
    owned = tokens // peers
    y, z, me = lax.axis_index("group"), lax.axis_index("ctx"), lax.axis_index("head")
    above, below = z + 1 < ctx, z > 0
    other = {"group": 1 - y} if share else None

    barrier = pltpu.get_barrier_semaphore()

    @pl.when(above)
    def _():
        pl.semaphore_signal(barrier, inc=1, device_id={"ctx": z + 1}, device_id_type=MESH)

    @pl.when(below)
    def _():
        pl.semaphore_signal(barrier, inc=1, device_id={"ctx": z - 1}, device_id_type=MESH)

    if share:
        pl.semaphore_signal(barrier, inc=1, device_id=other, device_id_type=MESH)
    for d in range(1, peers):
        pl.semaphore_signal(
            barrier, inc=1, device_id={"head": lax.rem(me + d, peers)}, device_id_type=MESH
        )
    ends = jnp.where(above, 1, 0) + jnp.where(below, 1, 0)
    pl.semaphore_wait(barrier, peers - 1 + (1 if share else 0) + ends)

    def line_chunk(i):
        return 2 * i + y if share else i

    def piece(j, c, r):
        return wg.at[j, c, rows_of(r, span)]

    def send(src, j, c, r, sem, target):
        return pltpu.make_async_remote_copy(
            src_ref=src,
            dst_ref=piece(j, c, r),
            send_sem=sem.at[j, c, r],
            recv_sem=w_recv.at[j, c, r],
            device_id=target,
            device_id_type=MESH,
        )

    def own_piece(c, r):
        return w_ref.at[rows_of(r, span), rows_of(c, cw)]

    def arrived(j, c, r):
        send(piece(j, c, r), j, c, r, up_send, {"head": lax.rem(me + 1, peers)}).wait_recv()

    own_count = line_chunks * PIECES
    early = jnp.where(z == ctx - 2, own_count * 3 // 8, 0)

    def own_send(i, flag, sem, target, wait=False):
        c, r = line_chunk(lax.div(i, PIECES)), lax.rem(i, PIECES)

        @pl.when(flag)
        def _():
            copy = send(own_piece(c, r), z, c, r, sem, {"ctx": target})
            if wait:
                copy.wait_send()
            else:
                copy.start()

    def own_down(i, wait=False):
        own_send(i, below, down_send, z - 1, wait)

    def own_up(i, first_part):
        now = (i < early) if first_part else (i >= early)
        own_send(i, jnp.logical_and(above, now), up_send, z + 1)

    def each(count, body):
        def go(i, carry):
            body(i)
            return carry

        lax.fori_loop(0, count, go, 0)

    each(own_count, own_down)
    each(own_count, lambda i: own_up(i, True))

    def local_copy(c):
        return pltpu.make_async_copy(w_ref.at[:, rows_of(c, cw)], wg.at[z, c], local_sem.at[c])

    each(chunks, lambda c: local_copy(c).start())

    late = jnp.where(z == ctx - 1, 0, DELAY)

    def service(at, wait=False):
        for up in (True, False):
            slot = at - late * PIECES if up and not wait else at
            fits = jnp.logical_and(slot >= 0, slot < slots)
            slot = jnp.where(fits, slot, 0)
            unit, r = lax.div(slot, PIECES), lax.rem(slot, PIECES)
            s, c = lax.div(unit, line_chunks), line_chunk(lax.rem(unit, line_chunks))
            if up:
                j, more, sem, target = z - 1 - s, above, up_send, z + 1
            else:
                j, more, sem, target = z + 1 + s, below, down_send, z - 1
            valid = jnp.logical_and(j >= 0, j < ctx)

            @pl.when(jnp.logical_and(valid, fits))
            def _():
                if not wait:
                    arrived(j, c, r)

                @pl.when(more)
                def _():
                    copy = send(piece(j, c, r), j, c, r, sem, {"ctx": target})
                    if wait:
                        copy.wait_send()
                    else:
                        copy.start()

                if share:
                    copy = send(piece(j, c, r), j, c, r, side_send, other)
                    if wait:
                        copy.wait_send()
                    else:
                        copy.start()

    spots = lax.broadcasted_iota(jnp.int32, (heads, width), 1)
    owner = lax.broadcasted_iota(jnp.int32, (heads, width), 0)
    inside = jnp.logical_and(spots >= owner * HEADP, spots < owner * HEADP + HEADP)
    expander[...] = jnp.where(inside, 1.0, 0.0).astype(BF16)

    def spread(v, lo, size):
        high = v.astype(BF16)
        low = (v - high.astype(F32)).astype(BF16)
        e = expander[:, lo : lo + size]
        return jnp.dot(high, e, preferred_element_type=F32) + jnp.dot(
            low, e, preferred_element_type=F32
        )

    row_i = lax.broadcasted_iota(jnp.int32, (STRETCH, STRETCH), 0)
    col_i = lax.broadcasted_iota(jnp.int32, (STRETCH, STRETCH), 1)
    lower = row_i >= col_i
    nt = (((1,), (1,)), ((), ()))
    tn = (((0,), (0,)), ((), ()))

    st[...] = jnp.zeros_like(st)

    def states(k, lead):
        rows = rows_of(k, STRETCH)
        low_tri = jnp.where(lower, 1.0, 0.0).astype(F32)
        eye = jnp.where(row_i == col_i, 1.0, 0.0).astype(F32)
        logd = jnp.log(dec_ref[:, rows])
        logs = jnp.log(step_ref[:, rows])
        exact = functools.partial(
            lax.dot_general,
            dimension_numbers=nt,
            precision=lax.Precision.HIGHEST,
            preferred_element_type=F32,
        )
        ramp = exact(logd, low_tri)
        rt = exact(low_tri, logd)
        st_t = exact(eye, logs)
        rows_r[k] = ramp - logs
        ramp_t[k] = rt
        lead_ref[k] = lead
        end = rt[STRETCH - 1 : STRETCH, :]
        tails = jnp.exp(end - (rt - st_t))
        total = jnp.broadcast_to(jnp.exp(end), (8, heads))
        for g in range(groups):
            cols = slice(g * gw, (g + 1) * gw)
            weighted = (x_ref[rows, cols].astype(F32) * spread(tails, g * gw, gw)).astype(BF16)
            made = lax.dot_general(
                bm_ref[rows, g * STATE : (g + 1) * STATE],
                weighted,
                tn,
                preferred_element_type=F32,
            )
            old = st[:, cols]
            ent[k, :, cols] = old.astype(BF16)
            st[:, cols] = spread(total, g * gw, gw)[0:1] * old + made
        return lead + jnp.broadcast_to(end, (8, heads))

    lead = lax.fori_loop(0, blocks, states, jnp.zeros((8, heads), F32))
    full_ref[...] = jnp.exp(lead)

    def state_copy(q):
        return pltpu.make_async_remote_copy(
            src_ref=sbuf.at[q],
            dst_ref=inc.at[q],
            send_sem=st_send.at[q],
            recv_sem=st_recv.at[q],
            device_id={"ctx": z + 1},
            device_id_type=MESH,
        )

    @pl.when(z == 0)
    def _():
        for q in range(QUARTERS):
            inc[q] = jnp.zeros_like(inc[q])
            sbuf[q] = st[:, q * qw : (q + 1) * qw].astype(BF16)

            @pl.when(above)
            def _():
                state_copy(q).start()

        each(own_count, lambda i: own_up(i, False))

    def chain():
        for q in range(QUARTERS):
            pltpu.make_async_remote_copy(
                src_ref=sbuf.at[q],
                dst_ref=inc.at[q],
                send_sem=st_send.at[q],
                recv_sem=st_recv.at[q],
                device_id={"ctx": z - 1},
                device_id_type=MESH,
            ).wait_recv()

            @pl.when(above)
            def _():
                fall = spread(full_ref[...], q * qw, qw)[0:1]
                held = st[:, q * qw : (q + 1) * qw]
                sbuf[q] = (fall * inc[q].astype(F32) + held).astype(BF16)
                state_copy(q).start()

    half = lax.broadcasted_iota(jnp.int32, (STRETCH, 2 * HEADP), 1) < HEADP
    keep_lo = jnp.where(half, 1.0, 0.0).astype(BF16)
    keep_hi = jnp.where(half, 0.0, 1.0).astype(BF16)
    per_group = heads // groups

    def own_block(k, carry):
        rows = rows_of(k, STRETCH)
        rt = ramp_t[k]
        rr = rows_r[k]
        entry = jnp.exp(rt)
        for g in range(groups):
            c_map = cm_ref[rows, g * STATE : (g + 1) * STATE]
            b_map = bm_ref[rows, g * STATE : (g + 1) * STATE]
            scores = lax.dot_general(c_map, b_map, nt, preferred_element_type=F32)
            cols = slice(g * gw, (g + 1) * gw)
            skip = spread(jnp.broadcast_to(skip_ref[...], (8, heads)), g * gw, gw)[0:1]
            y_ref[rows, cols] = (
                jnp.dot(c_map, ent[k, :, cols], preferred_element_type=F32)
                * spread(entry, g * gw, gw)
                + skip * x_ref[rows, cols].astype(F32)
            )
            for pair in range(per_group // 2):
                mixes = []
                for h in (g * per_group + 2 * pair, g * per_group + 2 * pair + 1):
                    fade = jnp.where(lower, rt[:, h : h + 1] - rr[h : h + 1, :], -1e30)
                    mixes.append((scores * jnp.exp(fade)).astype(BF16))
                at = slice(g * gw + pair * 2 * HEADP, g * gw + (pair + 1) * 2 * HEADP)
                both = x_ref[rows, at]
                y_ref[rows, at] += jnp.dot(
                    jnp.concatenate(mixes, axis=1),
                    jnp.concatenate([both * keep_lo, both * keep_hi], axis=0),
                    preferred_element_type=F32,
                )

        return carry

    lax.fori_loop(0, blocks, own_block, 0)
    service(0)
    service(1)

    @pl.when(below)
    def _():
        chain()
        each(own_count, lambda i: own_up(i, False))

    def finish_block(k, carry):
        rows = rows_of(k, STRETCH)
        reach = jnp.exp(ramp_t[k] + lead_ref[k, 0:1])
        squares = [jnp.zeros((STRETCH, 1), F32) for _ in range(groups)]
        for q in range(QUARTERS):
            g = q * qw // gw
            cols = slice(q * qw, (q + 1) * qw)
            carried = jnp.dot(
                cm_ref[rows, g * STATE : (g + 1) * STATE], inc[q], preferred_element_type=F32
            )
            gate = gate_ref[rows, cols].astype(F32)
            gated = (y_ref[rows, cols] + carried * spread(reach, q * qw, qw)) * (
                gate / (1.0 + jnp.exp(-gate))
            )
            y_ref[rows, cols] = gated
            squares[g] = squares[g] + jnp.sum(gated * gated, axis=1, keepdims=True)
        for g in range(groups):
            cols = slice(g * gw, (g + 1) * gw)
            factor = lax.rsqrt(squares[g] / gw + 1e-05)
            normed[rows, cols] = (y_ref[rows, cols] * factor * gain_ref[:, cols].astype(F32)).astype(
                BF16
            )

        service(2 + k)
        return carry

    lax.fori_loop(0, blocks, finish_block, 0)
    first = 2 + blocks

    def partial_copy(d, j, c):
        peer = lax.rem(me + d, peers)
        return pltpu.make_async_remote_copy(
            src_ref=part.at[j, c, rows_of(peer, owned)],
            dst_ref=rs.at[d - 1, j, c],
            send_sem=rs_send.at[d - 1, j, c],
            recv_sem=rs_recv.at[d - 1, j, c],
            device_id={"head": peer},
            device_id_type=MESH,
        )

    entries = max(chunks, 4 if share else 2)

    def locate(v, e):
        own = v == 0
        line = e < 2
        rising = lax.rem(e, 2) == 0
        unit = jnp.where(line, v - 1, v - 2) - jnp.where(rising, late, 0)
        known = jnp.logical_and(unit >= 0, unit < units)
        safe = jnp.where(known, unit, 0)
        s, i = lax.div(safe, line_chunks), lax.rem(safe, line_chunks)
        j = jnp.where(rising, z - 1 - s, z + 1 + s)
        if share:
            c = jnp.where(line, 2 * i + y, 2 * i + 1 - y)
        else:
            c = i
        known = jnp.logical_and(known, e < (4 if share else 2))
        known = jnp.logical_and(known, jnp.logical_and(j >= 0, j < ctx))
        valid = jnp.where(own, e < chunks, known)
        return own, line, jnp.where(own, z, j), jnp.where(own, e, c), valid

    def project(v, e):
        own, line, j, c, valid = locate(v, e)

        @pl.when(jnp.logical_and(valid, own))
        def _():
            local_copy(c).wait()

        @pl.when(jnp.logical_and(valid, jnp.logical_not(jnp.logical_or(own, line))))
        def _():
            for r in range(PIECES):
                arrived(j, c, r)

        @pl.when(valid)
        def _():
            part[j, c] = jnp.dot(normed[...], wg[j, c], preferred_element_type=F32).astype(BF16)
            for d in range(1, peers):
                partial_copy(d, j, c).start()

    def collect(v, e):
        own, line, j, c, valid = locate(v, e)

        @pl.when(valid)
        def _():
            total = part[j, c, rows_of(me, owned)].astype(F32)
            for d in range(1, peers):
                partial_copy(d, j, c).wait_recv()
                total = total + rs[d - 1, j, c].astype(F32)
            out_ref[:, rows_of(j * chunks + c, cw)] = total.astype(BF16)

    def rounds(v):
        @pl.when(jnp.logical_and(v >= 1, v <= units + DELAY))
        def _():
            for r in range(PIECES):
                slot = (v - 1) * PIECES + r

                @pl.when(slot >= first)
                def _():
                    service(slot)

        each(entries, lambda e: project(v, e))

    each(units + 2 + DELAY, rounds)
    each(units + 2 + DELAY, lambda v: each(entries, lambda e: collect(v, e)))

    each(own_count, lambda i: own_down(i, True))
    each(own_count, lambda i: own_send(i, above, up_send, z + 1, True))
    each(slots, lambda i: service(i, True))

    @pl.when(above)
    def _():
        for q in range(QUARTERS):
            state_copy(q).wait_send()

    def sent(u):
        j, c = lax.div(u, chunks), lax.rem(u, chunks)
        for d in range(1, peers):
            partial_copy(d, j, c).wait_send()

    each(ctx * chunks, sent)


def shards(
    sizes,
    head_input,
    gate_input,
    input_map,
    output_map,
    step_size,
    decays,
    bypass_scale,
    norm_gain,
    out_weight,
):
    lanes, ctx, peers = sizes
    tokens, width = head_input.shape
    heads = step_size.shape[0]
    blocks = tokens // STRETCH
    depth, cols = out_weight.shape
    cw = min(cols, 256)
    chunks = cols // cw
    owned = tokens // peers
    dma = pltpu.SemaphoreType.DMA
    vmem = pl.BlockSpec(memory_space=pltpu.VMEM)
    return pl.pallas_call(
        functools.partial(layer, sizes),
        out_shape=jax.ShapeDtypeStruct((owned, ctx * cols), BF16),
        in_specs=[vmem] * 8 + [pl.BlockSpec(memory_space=pl.ANY)],
        out_specs=vmem,
        scratch_shapes=[
            pltpu.VMEM((ctx, chunks, depth, cw), BF16),
            pltpu.VMEM((ctx, chunks, tokens, cw), BF16),
            pltpu.VMEM((peers - 1, ctx, chunks, owned, cw), BF16),
            pltpu.VMEM((tokens, width), F32),
            pltpu.VMEM((STATE, width), F32),
            pltpu.VMEM((blocks, STATE, width), BF16),
            pltpu.VMEM((QUARTERS, STATE, width // QUARTERS), BF16),
            pltpu.VMEM((QUARTERS, STATE, width // QUARTERS), BF16),
            pltpu.VMEM((tokens, width), BF16),
            pltpu.VMEM((heads, width), BF16),
            pltpu.VMEM((blocks, STRETCH, heads), F32),
            pltpu.VMEM((blocks, heads, STRETCH), F32),
            pltpu.VMEM((blocks, 8, heads), F32),
            pltpu.VMEM((8, heads), F32),
            dma((chunks,)),
            dma((ctx, chunks, PIECES)),
            dma((ctx, chunks, PIECES)),
            dma((ctx, chunks, PIECES)),
            dma((ctx, chunks, PIECES)),
            dma((QUARTERS,)),
            dma((QUARTERS,)),
            dma((peers - 1, ctx, chunks)),
            dma((peers - 1, ctx, chunks)),
        ],
        compiler_params=pltpu.CompilerParams(
            collective_id=0, has_side_effects=True, vmem_limit_bytes=60 << 20
        ),
    )(
        head_input,
        gate_input,
        input_map,
        output_map,
        step_size,
        decays,
        bypass_scale.reshape(1, heads),
        norm_gain.reshape(1, width),
        out_weight,
    )


def solution(mesh):
    sizes = (mesh.shape["group"], mesh.shape["ctx"], mesh.shape["head"])
    return jax.shard_map(
        functools.partial(shards, sizes),
        mesh=mesh,
        in_specs=(
            P(("group", "ctx"), "head"),
            P(("group", "ctx"), "head"),
            P(("group", "ctx"), "head"),
            P(("group", "ctx"), "head"),
            P("head", ("group", "ctx")),
            P("head", ("group", "ctx")),
            P("head"),
            P("head"),
            P("head", "ctx"),
        ),
        out_specs=P(("group", "ctx", "head"), None),
        check_vma=False,
    )
```
